128 devices in a mesh: tm: 4 (over x), op: 32 (over y, z, core).
Axes of the slice: x: 4, y: 4, z: 4, core: 2. Of those that a mesh axis runs over, the one named last changes fastest.
Arguments:
- sink_elem: bfloat16 [2, 4, 2048, 16384], P(None, 'tm', 'op'), may hold values from -6 to 6
- source_elem: bfloat16 [2, 2, 2048, 16384], P(None, None, None, 'op'), may hold values from -6 to 6
- peram: bfloat16 [2, 4, 2, 512, 512], P(None, 'tm', None, 'op'), may hold values from -4 to 4
- pair_list: int32 [16, 1], replicated, may hold values from 0 to 15
- spin_sets: int32 [16, 3], replicated, may hold values from 0 to 3
Outputs:
- correlator: float32 [2, 4, 2, 16, 1], P(None, 'tm')
The draws below stay inside these ranges and needn't reach their ends.
All inputs are finite; a program needn't handle non-finite values.
Results may differ from the reference program's by a relative error of at most 0.0041.
Values may be sent and summed in bfloat16 or wider, within the bound.
A program may use at most 192 MiB of HBM per device.

```python
import jax
import jax.numpy as jnp
from jax import lax

NEV = 128
NSPIN = 4
NOP = 16
TSRC = 2
PAIRS = 1
TSNK = 4


def plant(entries, stream_key, smallest, top_value):
    longest = entries.shape.index(max(entries.shape))
    spots = []
    for shift in (0, 1):
        where = [jax.random.randint(jax.random.fold_in(stream_key, axis), (), 0, length) for axis, length in enumerate(entries.shape)]
        where[longest] = (where[longest] + shift) % entries.shape[longest]
        spots.append(tuple(where))
    return entries.at[spots[0]].set(smallest).at[spots[1]].set(top_value)


def block_levels(key, shape, cuts, low, high):
    level = 1.0
    for position, shards_of in cuts:
        draws = jax.random.uniform(jax.random.fold_in(jax.random.fold_in(key, 6), position), (shards_of,), jnp.float32, low / len(cuts), high / len(cuts))
        level = level * jnp.repeat(jnp.exp(draws), shape[position] // shards_of).reshape((-1,) + (1,) * (len(shape) - 1 - position))
    return level


def gaussian(stream_key, dims, deviation, most, shards=(), held_as=jnp.bfloat16):
    loudness = block_levels(stream_key, dims, shards, -0.22, 0.18) if shards else 1.0
    result = jax.random.normal(stream_key, dims, jnp.float32) * deviation * loudness
    return jnp.minimum(jnp.maximum(result, -most), most).astype(held_as)


def setup_inputs(seed: int = 0) -> dict:
    keys = jax.random.split(jax.random.key(seed), 6)
    return {
        "sink_elem": gaussian(keys[0], (2, TSNK, NOP * NEV, NEV * NEV), 1.0, 6.0, ((1, 4), (2, 32))),
        "source_elem": gaussian(keys[1], (2, TSRC, NOP * NEV, NEV * NEV), 1.0, 6.0, ((3, 32),)),
        "peram": gaussian(keys[2], (2, TSNK, TSRC, NSPIN * NEV, NSPIN * NEV), 0.5, 4.0, ((1, 4), (3, 32))),
        "pair_list": plant(jax.random.randint(keys[3], (NOP, PAIRS), 0, NOP), jax.random.fold_in(keys[3], 1), 0, NOP - 1).astype(jnp.int32),
        "spin_sets": plant(jax.random.randint(keys[4], (NOP, 3), 0, NSPIN), jax.random.fold_in(keys[4], 1), 0, NSPIN - 1).astype(jnp.int32),
    }


def keep_bf16(value):
    return lax.optimization_barrier(value.astype(jnp.bfloat16)).astype(jnp.float32)


def reference(sink_elem, source_elem, peram, pair_list, spin_sets):
    results = []
    for t in range(TSNK):
        phi = sink_elem[:, t].astype(jnp.float32).reshape(2, NOP, NEV * NEV, NEV)
        per_time = []
        for t0 in range(TSRC):
            blocks = peram[:, t, t0].astype(jnp.float32).reshape(2, NSPIN, NEV, NSPIN, NEV)
            blocks = jnp.transpose(blocks, (1, 3, 0, 2, 4))
            source = source_elem[:, t0].astype(jnp.float32).reshape(2, NOP, NEV, NEV * NEV)
            per_slot = []
            for p in range(PAIRS):
                other = pair_list[:, p]
                third = blocks[spin_sets[:, 2], spin_sets[other, 2]]
                second = blocks[spin_sets[:, 1], spin_sets[other, 1]]
                first = blocks[spin_sets[:, 0], spin_sets[other, 0]]

                def kmode(a, b):
                    return jnp.einsum('oxk,okb->oxb', a, b)

                x_re = kmode(phi[0], third[:, 0]) - kmode(phi[1], third[:, 1])
                x_im = kmode(phi[0], third[:, 1]) + kmode(phi[1], third[:, 0])
                x_re = keep_bf16(x_re).reshape(NOP, NEV, NEV, NEV)
                x_im = keep_bf16(x_im).reshape(NOP, NEV, NEV, NEV)

                def jmode(a, b):
                    return jnp.einsum('oijk,ojb->oibk', a, b)

                y_re = jmode(x_re, second[:, 0]) - jmode(x_im, second[:, 1])
                y_im = jmode(x_re, second[:, 1]) + jmode(x_im, second[:, 0])
                y_re = keep_bf16(y_re).reshape(NOP, NEV, NEV * NEV)
                y_im = keep_bf16(y_im).reshape(NOP, NEV, NEV * NEV)
                chosen = jnp.take(source, other, axis=1)

                def inner(a, b):
                    return jnp.einsum('oic,ojc->oij', a, b)

                m_re = inner(y_re, chosen[0]) + inner(y_im, chosen[1])
                m_im = inner(y_im, chosen[0]) - inner(y_re, chosen[1])
                c_re = jnp.sum(first[:, 0] * m_re - first[:, 1] * m_im, axis=(1, 2))
                c_im = jnp.sum(first[:, 0] * m_im + first[:, 1] * m_re, axis=(1, 2))
                per_slot.append(jnp.stack([c_re, c_im]))
            per_time.append(jnp.stack(per_slot, axis=-1))
        results.append(jnp.stack(per_time, axis=1))
    return jnp.stack(results, axis=1) * (1.0 / float(NEV ** 3))
```

```python
import functools

import jax
import jax.numpy as jnp
from jax import lax
from jax.experimental import pallas as pl
from jax.experimental.pallas import tpu as pltpu
from jax.sharding import PartitionSpec as P

NEV = 128
NOP = 16
TSRC = 2
MESH = pl.DeviceIdType.MESH
BF16 = jnp.bfloat16
F32 = jnp.float32

ORDER = [
    (0, 1), (1, 0), (0, 3), (3, 0), (1, 1), (3, 3), (1, 3), (3, 1),
    (2, 0), (0, 2), (2, 2), (1, 2), (2, 1), (3, 2), (2, 3),
]
PACKED_Y = sum(dy * 4**k for k, (dy, dz) in enumerate(ORDER))
PACKED_Z = sum(dz * 4**k for k, (dy, dz) in enumerate(ORDER))


def kernel(
    pair_ref, spin_ref, sink, source, peram, out,
    phi, sown, ssib, sbuf, rown, rnb, taub, xbuf, ybuf, pacc, t2m, t3m, mine, other, res,
    lsem, bsend, brecv, tsend, trecv, ssem, rsem, xsend, xrecv, fsend, frecv,
):
    t, o = lax.axis_index("tm"), lax.axis_index("op")
    h, chip = lax.rem(o, 2), lax.div(o, 2)
    y, z = lax.div(chip, 4), lax.rem(chip, 4)
    par = lax.rem(t, 2)
    sibling = (t, o + 1 - 2 * h)

    def at(y2, z2):
        return (t, (y2 * 4 + z2) * 2 + h)

    def beside(g):
        return (lax.rem(t + (1 - 2 * par) * (1 - 2 * g) + 4, 4), o)

    def remote(src, dst, send, recv, device):
        return pltpu.make_async_remote_copy(
            src_ref=src, dst_ref=dst, send_sem=send, recv_sem=recv, device_id=device, device_id_type=MESH
        )

    half = pl.ds(pl.multiple_of(par * 256, 256), 256)
    my_rows = pl.ds(pl.multiple_of(h * 64, 64), 64)

    local = []
    my_tau = pl.ds(pl.multiple_of(h * 16, 16), 16)
    for c in range(2):
        local.append(pltpu.make_async_copy(source.at[c, h, :, :, half], sown.at[c], lsem.at[c]))
    for c in range(2):
        local.append(pltpu.make_async_copy(sink.at[c, 0], phi.at[c, my_rows], lsem.at[2 + c]))
    for c in range(2):
        for b in range(4):
            local.append(
                pltpu.make_async_copy(
                    peram.at[c, 0, h, :, b * NEV : (b + 1) * NEV], taub.at[c, b, y, z, my_tau], lsem.at[4 + 4 * c + b]
                )
            )
    for copy in local:
        copy.start()

    barrier = pltpu.get_barrier_semaphore()

    def greet(k, carry):
        other_chip = lax.rem(chip + k, 16)
        pl.semaphore_signal(barrier, inc=1, device_id=(t, other_chip * 2 + h), device_id_type=MESH)
        return carry

    lax.fori_loop(1, 16, greet, 0)
    pl.semaphore_signal(barrier, inc=1, device_id=sibling, device_id_type=MESH)
    for g in range(2):
        pl.semaphore_signal(barrier, inc=1, device_id=beside(g), device_id_type=MESH)
    pl.semaphore_wait(barrier, 18)

    across = []
    for c in range(2):
        across.append(remote(source.at[c, 1 - h, :, :, half], ssib.at[c], bsend.at[c], brecv.at[c], sibling))
    for c in range(2):
        across.append(remote(sink.at[c, 0], phi.at[c, my_rows], bsend.at[2 + c], brecv.at[2 + c], sibling))
    for c in range(2):
        for b in range(4):
            n = 4 + 4 * c + b
            across.append(
                remote(
                    peram.at[c, 0, 1 - h, :, b * NEV : (b + 1) * NEV], taub.at[c, b, y, z, my_tau],
                    bsend.at[n], brecv.at[n], sibling,
                )
            )
    for copy in across[4:] + across[:4]:
        copy.start()

    for n in range(4, 12):
        local[n].wait()
        across[n].wait_recv()
    first, second = [], []
    for d in range(1, 4):
        y2, z2 = lax.rem(y + d, 4), lax.rem(z + d, 4)
        first.append(remote(taub.at[0, :, y, z], taub.at[0, :, y, z], tsend.at[d - 1], trecv.at[d - 1], at(y, z2)))
        first.append(remote(taub.at[1, :, y, z], taub.at[1, :, y, z], tsend.at[d + 2], trecv.at[d + 2], at(y2, z)))
        second.append(remote(taub.at[0, :, y], taub.at[0, :, y], tsend.at[d + 5], trecv.at[d + 5], at(y2, z)))
        second.append(remote(taub.at[1, :, :, z], taub.at[1, :, :, z], tsend.at[d + 8], trecv.at[d + 8], at(y, z2)))
    for copy in first:
        copy.start()

    def hand_on(slot, g):
        return remote(rown.at[slot], rnb.at[slot], xsend.at[slot], xrecv.at[slot], beside(g))

    def serve(p, tiles, g, begin, end, carry):
        def step(k, carry):
            cy, cz = carry
            target = lax.rem(y + lax.rem(cy, 4), 4) * 4 + lax.rem(z + lax.rem(cz, 4), 4)
            q = pair_ref[0, target]
            for c in range(2):
                sbuf[p * 15 + k, c] = tiles[c, q]
            send(p, k, target, g).start()
            return lax.div(cy, 4), lax.div(cz, 4)

        return lax.fori_loop(begin, end, step, carry)

    def send(p, k, target, g):
        return remote(
            sbuf.at[p * 15 + k], rown.at[chip * 2 + g], ssem.at[p * 15 + k], rsem.at[chip * 2 + g], (t, target * 2 + h)
        )

    def keep(tiles, g):
        q = pair_ref[0, chip]
        for c in range(2):
            rown[chip * 2 + g, c] = tiles[c, q]
        hand_on(chip * 2 + g, g).start()

    start = (jnp.int32(PACKED_Y), jnp.int32(PACKED_Z))
    for c in range(2):
        local[c].wait()
    carry = serve(0, sown, h, 0, 4, start)
    for copy in first:
        copy.wait_recv()
    for copy in second:
        copy.start()
    keep(sown, h)
    serve(0, sown, h, 4, 15, carry)
    for c in range(2):
        across[c].wait_recv()
    serve(1, ssib, 1 - h, 0, 15, start)
    keep(ssib, 1 - h)

    theirs = pair_ref[0, chip]
    for copy in second:
        copy.wait_recv()

    def block(c, n):
        left, right = spin_ref[n, chip], spin_ref[n, theirs]
        return taub[c, right, left].reshape(NEV, NEV)

    third_re, third_im = block(0, 2), block(1, 2)
    t3m[...] = jnp.concatenate(
        [jnp.concatenate([third_re, third_im], axis=1), jnp.concatenate([-third_im, third_re], axis=1)], axis=0
    )
    second_re, second_im = block(0, 1).astype(F32).T, block(1, 1).astype(F32).T
    t2m[...] = jnp.concatenate(
        [jnp.concatenate([second_re, -second_im], axis=1), jnp.concatenate([second_im, second_re], axis=1)], axis=0
    ).astype(BF16)
    for c in range(2):
        local[2 + c].wait()
        across[2 + c].wait_recv()

    def sender(carry):
        cy, cz = carry
        from_chip = lax.rem(y + 4 - lax.rem(cy, 4), 4) * 4 + lax.rem(z + 4 - lax.rem(cz, 4), 4)
        return from_chip, (lax.div(cy, 4), lax.div(cz, 4))

    def arrived(slot):
        remote(rown.at[slot], rown.at[slot], xsend.at[slot], rsem.at[slot], sibling).wait_recv()

    def take_and_hand_on(slot, g):
        arrived(slot)
        hand_on(slot, g).start()

    def rows16(ic, carry):
        i0 = pl.multiple_of(ic * 16, 16)

        def x_step(jb, inner):
            rows = []
            for jj in range(16):
                cols = pl.ds(pl.multiple_of((jb * 16 + jj) * NEV, NEV), NEV)
                rows.append(jnp.concatenate([phi[c, pl.ds(i0, 16), cols] for c in range(2)], axis=1))
            x = jnp.dot(jnp.concatenate(rows, axis=0), t3m[...], preferred_element_type=F32)
            place = pl.ds(pl.multiple_of(jb * 256, 256), 256)
            xbuf[0, place, :] = x[:, :NEV]
            xbuf[1, place, :] = x[:, NEV:]
            return inner

        lax.fori_loop(0, 8, x_step, 0)

        def y_step(ip, inner):
            parts = []
            for c in range(2):
                parts.append(
                    jnp.concatenate(
                        [xbuf[c, pl.ds(2 * ip + e, NEV, stride=16), :].astype(BF16) for e in range(2)], axis=1
                    )
                )
            value = jnp.dot(t2m[...], jnp.concatenate(parts, axis=0), preferred_element_type=F32)
            for e in range(2):
                place = pl.ds(pl.multiple_of((ic * 16 + 2 * ip + e) * 256, 256), 256)
                ybuf[place, :] = value[:, e * NEV : (e + 1) * NEV]
            return inner

        lax.fori_loop(0, 8, y_step, 0)
        for r in range(2):
            from_chip, later = sender(carry)
            slot = from_chip * 2 + h

            @pl.when(ic * 2 + r < 15)
            def _go():
                take_and_hand_on(slot, h)

            carry = later
        return carry

    lax.fori_loop(0, 8, rows16, start)

    pacc[...] = jnp.zeros_like(pacc)

    def contract(tile, slot, parity):
        first_j = slot * 4 + 2 * parity
        parts = []
        for c in range(2):
            parts.append(
                jnp.concatenate(
                    [ybuf[pl.ds(c * NEV + first_j + jj, NEV, stride=256), :].astype(BF16) for jj in range(2)], axis=1
                )
            )
        left = jnp.concatenate(parts, axis=0)
        right = tile[slot].reshape(2 * NEV, 256)
        pacc[...] += lax.dot_general(left, right, (((1,), (1,)), ((), ())), preferred_element_type=F32)

    def handed(slot):
        remote(rnb.at[slot], rnb.at[slot], xsend.at[slot], xrecv.at[slot], sibling).wait_recv()
        contract(rnb, slot, 1 - par)

    def main(k, carry):
        from_chip, carry = sender(carry)
        take_and_hand_on(from_chip * 2 + 1 - h, 1 - h)
        contract(rown, from_chip * 2 + h, par)
        contract(rown, from_chip * 2 + 1 - h, par)
        handed(from_chip * 2 + h)
        return carry

    contract(rown, chip * 2 + h, par)
    contract(rown, chip * 2 + 1 - h, par)
    lax.fori_loop(0, 15, main, start)
    handed(chip * 2 + h)
    handed(chip * 2 + 1 - h)

    def tail(k, carry):
        from_chip, carry = sender(carry)
        handed(from_chip * 2 + 1 - h)
        return carry

    lax.fori_loop(0, 15, tail, start)

    first_re, first_im = block(0, 0).astype(F32), block(1, 0).astype(F32)
    m_re = pacc[:NEV, :NEV] + pacc[NEV:, NEV:]
    m_im = pacc[NEV:, :NEV] - pacc[:NEV, NEV:]

    def total(v):
        return jnp.sum(jnp.sum(v, axis=0, keepdims=True), axis=1, keepdims=True) * (1.0 / float(NEV**3))

    c_re, c_im = total(first_re * m_re - first_im * m_im), total(first_re * m_im + first_im * m_re)
    row = lax.broadcasted_iota(jnp.int32, (8, NEV), 0)
    zero = jnp.zeros((8, NEV), F32)
    mine[...] = jnp.where(row == h, zero + c_re, jnp.where(row == 2 + h, zero + c_im, zero))
    swap = remote(mine, other, fsend.at[15], frecv.at[16], sibling)
    swap.start()
    swap.wait()
    res[chip] = mine[...] + other[...]

    def share(k):
        target = lax.rem(chip + k, 16)
        return remote(res.at[chip], res.at[chip], fsend.at[k - 1], frecv.at[chip], (t, target * 2 + h))

    def share_start(k, carry):
        share(k).start()
        return carry

    lax.fori_loop(1, 16, share_start, 0)

    def share_wait(k, carry):
        who = lax.rem(chip + k, 16)
        share(k).wait_send()
        remote(res.at[who], res.at[who], fsend.at[k - 1], frecv.at[who], sibling).wait_recv()
        return carry

    lax.fori_loop(1, 16, share_wait, 0)
    lane = lax.broadcasted_iota(jnp.int32, (8, NEV), 1)
    gathered = zero
    for n in range(NOP):
        gathered = jnp.where(lane == n, res[n], gathered)
    out[...] = gathered

    for copy in across + first + second:
        copy.wait_send()

    def drain_sends(k, carry):
        remote(sbuf.at[k], sbuf.at[k], ssem.at[k], xrecv.at[0], sibling).wait_send()
        return carry

    lax.fori_loop(0, 30, drain_sends, 0)

    def drain_hands(k, carry):
        remote(rown.at[k], rown.at[k], xsend.at[k], xrecv.at[0], sibling).wait_send()
        return carry

    lax.fori_loop(0, 32, drain_hands, 0)


def on_device(sink_elem, source_elem, peram, pair_list, spin_sets):
    gathered = pl.pallas_call(
        kernel,
        name="correlate",
        out_shape=jax.ShapeDtypeStruct((8, NEV), F32),
        in_specs=[
            pl.BlockSpec(memory_space=pltpu.SMEM),
            pl.BlockSpec(memory_space=pltpu.SMEM),
            pl.BlockSpec(memory_space=pl.ANY),
            pl.BlockSpec(memory_space=pl.ANY),
            pl.BlockSpec(memory_space=pl.ANY),
        ],
        out_specs=pl.BlockSpec(memory_space=pltpu.VMEM),
        scratch_shapes=[
            pltpu.VMEM((2, NEV, NEV * NEV), BF16),
            pltpu.VMEM((2, NOP, NEV, 256), BF16),
            pltpu.VMEM((2, NOP, NEV, 256), BF16),
            pltpu.VMEM((30, 2, NEV, 256), BF16),
            pltpu.VMEM((32, 2, NEV, 256), BF16),
            pltpu.VMEM((32, 2, NEV, 256), BF16),
            pltpu.VMEM((2, 4, 4, 4, 32, NEV), BF16),
            pltpu.VMEM((2, 16 * NEV, NEV), F32),
            pltpu.VMEM((2 * NEV * NEV, NEV), F32),
            pltpu.VMEM((2 * NEV, 2 * NEV), F32),
            pltpu.VMEM((2 * NEV, 2 * NEV), BF16),
            pltpu.VMEM((2 * NEV, 2 * NEV), BF16),
            pltpu.VMEM((8, NEV), F32),
            pltpu.VMEM((8, NEV), F32),
            pltpu.VMEM((NOP, 8, NEV), F32),
            pltpu.SemaphoreType.DMA((12,)),
            pltpu.SemaphoreType.DMA((12,)),
            pltpu.SemaphoreType.DMA((12,)),
            pltpu.SemaphoreType.DMA((12,)),
            pltpu.SemaphoreType.DMA((12,)),
            pltpu.SemaphoreType.DMA((30,)),
            pltpu.SemaphoreType.DMA((32,)),
            pltpu.SemaphoreType.DMA((32,)),
            pltpu.SemaphoreType.DMA((32,)),
            pltpu.SemaphoreType.DMA((16,)),
            pltpu.SemaphoreType.DMA((17,)),
        ],
        compiler_params=pltpu.CompilerParams(
            collective_id=0, has_side_effects=True, vmem_limit_bytes=56 * 2**20
        ),
    )(pair_list.T, spin_sets.T, sink_elem, source_elem.reshape(2, TSRC, NOP, NEV, source_elem.shape[3]), peram)
    return gathered[:4, :NOP].reshape(2, 1, TSRC, NOP, 1)


def solution(mesh):
    in_specs = (
        P(None, "tm", "op", None),
        P(None, None, None, "op"),
        P(None, "tm", None, "op", None),
        P(),
        P(),
    )
    out_specs = P(None, "tm", None, None, None)
    return jax.shard_map(on_device, mesh=mesh, in_specs=in_specs, out_specs=out_specs, check_vma=False)
```

```python
import functools

import jax
import jax.numpy as jnp
from jax import lax
from jax.experimental import pallas as pl
from jax.experimental.pallas import tpu as pltpu
from jax.sharding import PartitionSpec as P

NEV = 128
NOP = 16
TSRC = 2
MESH = pl.DeviceIdType.MESH
BF16 = jnp.bfloat16
F32 = jnp.float32

XJ = 64
YP = 4
OUT = 12
EARLY = (4, 4)

ORDER = [
    (0, 1), (1, 0), (0, 3), (3, 0), (1, 1), (3, 3), (1, 3), (3, 1),
    (2, 0), (0, 2), (2, 2), (1, 2), (2, 1), (3, 2), (2, 3),
]
PACKED_Y = sum(dy * 4**k for k, (dy, dz) in enumerate(ORDER))
PACKED_Z = sum(dz * 4**k for k, (dy, dz) in enumerate(ORDER))


def kernel(
    pair_ref, spin_ref, sink, source, peram, out,
    phi, sown, ssib, sbuf, rown, rnb, taub, tout, tsel, xbuf, ybuf, pacc, t2m, t3m, mine, other, res,
    lsem, bsend, brecv, tsend, trecv, ssem, rsem, xsend, xrecv, fsend, frecv,
):
    t, o = lax.axis_index("tm"), lax.axis_index("op")
    h, chip = lax.rem(o, 2), lax.div(o, 2)
    y, z = lax.div(chip, 4), lax.rem(chip, 4)
    par = lax.rem(t, 2)
    sibling = (t, o + 1 - 2 * h)

    def at(y2, z2):
        return (t, (y2 * 4 + z2) * 2 + h)

    def beside(g):
        return (lax.rem(t + (1 - 2 * par) * (1 - 2 * g) + 4, 4), o)

    def remote(src, dst, send, recv, device):
        return pltpu.make_async_remote_copy(
            src_ref=src, dst_ref=dst, send_sem=send, recv_sem=recv, device_id=device, device_id_type=MESH
        )

    my_rows = pl.ds(pl.multiple_of(h * 64, 64), 64)

    local = []
    my_tau = pl.ds(pl.multiple_of(h * 16, 16), 16)
    for c in range(2):
        some = pl.ds(c * 8, 8)
        local.append(pltpu.make_async_copy(source.at[par, h, some], sown.at[some], lsem.at[c]))
    for c in range(2):
        local.append(pltpu.make_async_copy(sink.at[c, 0], phi.at[c, my_rows], lsem.at[2 + c]))
    for c in range(2):
        for b in range(4):
            local.append(
                pltpu.make_async_copy(
                    peram.at[c, 0, h, :, b * NEV : (b + 1) * NEV], taub.at[c, b, y, my_tau], lsem.at[4 + 4 * c + b]
                )
            )
    for copy in local:
        copy.start()

    barrier = pltpu.get_barrier_semaphore()

    def greet(k, carry):
        other_chip = lax.rem(chip + k, 16)
        pl.semaphore_signal(barrier, inc=1, device_id=(t, other_chip * 2 + h), device_id_type=MESH)
        return carry

    lax.fori_loop(1, 16, greet, 0)
    pl.semaphore_signal(barrier, inc=1, device_id=sibling, device_id_type=MESH)
    for g in range(2):
        pl.semaphore_signal(barrier, inc=1, device_id=beside(g), device_id_type=MESH)
    pl.semaphore_wait(barrier, 18)

    across = []
    for c in range(2):
        some = pl.ds(c * 8, 8)
        across.append(remote(source.at[par, 1 - h, some], ssib.at[some], bsend.at[c], brecv.at[c], sibling))
    for c in range(2):
        across.append(remote(sink.at[c, 0], phi.at[c, my_rows], bsend.at[2 + c], brecv.at[2 + c], sibling))
    for c in range(2):
        for b in range(4):
            n = 4 + 4 * c + b
            across.append(
                remote(
                    peram.at[c, 0, 1 - h, :, b * NEV : (b + 1) * NEV], taub.at[c, b, y, my_tau],
                    bsend.at[n], brecv.at[n], sibling,
                )
            )
    for copy in across[4:] + across[:4]:
        copy.start()

    first, second = [], []
    for d in range(1, 4):
        y2, z2 = lax.rem(y + d, 4), lax.rem(z + d, 4)
        first.append(remote(taub.at[:, :, y], taub.at[:, :, y], tsend.at[d - 1], trecv.at[d - 1], at(y2, z)))
        second.append(remote(tout.at[d - 1], tsel.at[:, :, z], tsend.at[d + 2], trecv.at[d + 2], at(y, z2)))

    def spread_rows():
        for n in range(4, 12):
            local[n].wait()
            across[n].wait_recv()
        for copy in first:
            copy.start()

    def pick(d, n, c):
        target = y * 4 + lax.rem(z + d, 4)
        return taub[c, spin_ref[n, pair_ref[0, target]], spin_ref[n, target]]

    def spread_blocks():
        for copy in first:
            copy.wait_recv()
        for d in range(1, 4):
            for n in range(3):
                for c in range(2):
                    tout[d - 1, n, c] = pick(d, n, c)
            second[d - 1].start()
        for n in range(3):
            for c in range(2):
                tsel[n, c, z] = pick(0, n, c)

    def hand_on(slot, g):
        return remote(rown.at[slot], rnb.at[slot], xsend.at[slot], xrecv.at[slot], beside(g))

    def advance(order):
        return tuple(lax.div(digits, 4) + lax.rem(digits, 4) * 4**14 for digits in order)

    def half_of(m):
        return lax.rem(h + lax.div(m, 15), 2)

    def serve(m, order):
        target = lax.rem(y + lax.rem(order[0], 4), 4) * 4 + lax.rem(z + lax.rem(order[1], 4), 4)
        q = pair_ref[0, target]

        @pl.when(m < 15)
        def _own():
            sbuf[m] = sown[q]

        @pl.when(m >= 15)
        def _sib():
            sbuf[m] = ssib[q]

        place = chip * 2 + half_of(m)
        remote(sbuf.at[m], rown.at[place], ssem.at[m], rsem.at[place], (t, target * 2 + h)).start()
        return advance(order)

    def keep(p, tiles):
        q = pair_ref[0, chip]
        g = lax.rem(h + p, 2)
        rown[chip * 2 + g] = tiles[q]
        hand_on(chip * 2 + g, g).start()

    def slot_of(m, order):
        from_y, from_z = lax.rem(y + 4 - lax.rem(order[0], 4), 4), lax.rem(z + 4 - lax.rem(order[1], 4), 4)
        return (from_y * 4 + from_z) * 2 + half_of(m)

    def pump(n, orders):
        coming, going = orders
        slot = slot_of(n, coming)
        remote(rown.at[slot], rown.at[slot], xsend.at[slot], rsem.at[slot], sibling).wait_recv()
        hand_on(slot, half_of(n)).start()

        @pl.when(n < 30 - OUT)
        def _more():
            serve(n + OUT, going)

        return advance(coming), advance(going)

    start = (jnp.int32(PACKED_Y), jnp.int32(PACKED_Z))
    for c in range(2):
        local[c].wait()
    keep(0, sown)
    going = lax.fori_loop(0, OUT, serve, start)
    spread_rows()
    for c in range(2):
        across[c].wait_recv()
    keep(1, ssib)
    orders = lax.fori_loop(0, EARLY[0], pump, (start, going))
    spread_blocks()
    orders = lax.fori_loop(EARLY[0], EARLY[0] + EARLY[1], pump, orders)

    for copy in second:
        copy.wait_recv()

    def block(c, n):
        return tsel[n, c].reshape(NEV, NEV)

    third_re, third_im = block(0, 2), block(1, 2)
    t3m[...] = jnp.concatenate(
        [jnp.concatenate([third_re, third_im], axis=1), jnp.concatenate([-third_im, third_re], axis=1)], axis=0
    )
    second_re, second_im = block(0, 1).astype(F32).T, block(1, 1).astype(F32).T
    t2m[...] = jnp.concatenate(
        [jnp.concatenate([second_re, -second_im], axis=1), jnp.concatenate([second_im, second_re], axis=1)], axis=0
    ).astype(BF16)
    for c in range(2):
        local[2 + c].wait()
        across[2 + c].wait_recv()

    def rows16(ic, orders):
        n = EARLY[0] + EARLY[1] + ic * 2
        i0 = pl.multiple_of(ic * 16, 16)

        def x_step(jb, inner):
            rows = []
            for jj in range(XJ):
                cols = pl.ds(pl.multiple_of((jb * XJ + jj) * NEV, NEV), NEV)
                rows.append(jnp.concatenate([phi[c, pl.ds(i0, 16), cols] for c in range(2)], axis=1))
            x = jnp.dot(jnp.concatenate(rows, axis=0), t3m[...], preferred_element_type=F32)
            place = pl.ds(pl.multiple_of(jb * (XJ * 16), XJ * 16), XJ * 16)
            xbuf[0, place, :] = x[:, :NEV]
            xbuf[1, place, :] = x[:, NEV:]
            return inner

        lax.fori_loop(0, NEV // XJ, x_step, 0)
        orders = pump(n, orders)

        def y_step(iq, inner):
            for ip in range(YP):
                first_i = iq * (2 * YP) + 2 * ip
                parts = []
                for c in range(2):
                    parts.append(
                        jnp.concatenate(
                            [xbuf[c, pl.ds(first_i + e, NEV, stride=16), :].astype(BF16) for e in range(2)], axis=1
                        )
                    )
                value = jnp.dot(t2m[...], jnp.concatenate(parts, axis=0), preferred_element_type=F32)
                for e in range(2):
                    place = pl.ds(pl.multiple_of((ic * 16 + first_i + e) * 256, 256), 256)
                    ybuf[place, :] = value[:, e * NEV : (e + 1) * NEV]
            return inner

        lax.fori_loop(0, 8 // YP, y_step, 0)
        return pump(n + 1, orders)

    orders = lax.fori_loop(0, 8, rows16, orders)

    def contract(slots):
        left, right = [[], []], [[], []]
        for slot in slots:
            for c in range(2):
                for jj in range(4):
                    left[c].append(ybuf[pl.ds(c * NEV + slot * 4 + jj, NEV, stride=256), :].astype(BF16))
            right[0].append(rown[slot])
            right[1].append(rnb[slot])
        left, right = (
            jnp.concatenate([jnp.concatenate(part, axis=1) for part in parts], axis=0) for parts in (left, right)
        )
        return lax.dot_general(left, right, (((1,), (1,)), ((), ())), preferred_element_type=F32)

    def handed(slot):
        remote(rnb.at[slot], rnb.at[slot], xsend.at[slot], xrecv.at[slot], sibling).wait_recv()

    own, nxt = chip * 2 + h, chip * 2 + 1 - h
    handed(own)
    handed(nxt)
    pacc[...] = contract([own, nxt])

    def main(k, carry):
        orders, order = carry
        n = EARLY[0] + EARLY[1] + 16 + k

        @pl.when(n < 30)
        def _last():
            pump(n, orders)

        a, order = slot_of(2 * k, order), advance(order)
        b, order = slot_of(2 * k + 1, order), advance(order)
        handed(a)
        handed(b)
        pacc[...] += contract([a, b])
        return (advance(orders[0]), advance(orders[1])), order

    lax.fori_loop(0, 15, main, (orders, start))

    for copy in across + first + second:
        copy.wait_send()

    def drain_sends(k, inner):
        remote(sbuf.at[k], sbuf.at[k], ssem.at[k], xrecv.at[0], sibling).wait_send()
        return inner

    lax.fori_loop(0, 30, drain_sends, 0)

    first_re, first_im = block(0, 0).astype(F32), block(1, 0).astype(F32)
    fetched, given = pacc[:, :NEV], pacc[:, NEV:]
    with_re, with_im = jnp.where(par == 0, fetched, given), jnp.where(par == 0, given, fetched)
    m_re = with_re[:NEV] + with_im[NEV:]
    m_im = with_re[NEV:] - with_im[:NEV]

    def total(v):
        return jnp.sum(jnp.sum(v, axis=0, keepdims=True), axis=1, keepdims=True) * (1.0 / float(NEV**3))

    c_re, c_im = total(first_re * m_re - first_im * m_im), total(first_re * m_im + first_im * m_re)
    row = lax.broadcasted_iota(jnp.int32, (8, NEV), 0)
    zero = jnp.zeros((8, NEV), F32)
    mine[...] = jnp.where(row == h, zero + c_re, jnp.where(row == 2 + h, zero + c_im, zero))
    swap = remote(mine, other, fsend.at[15], frecv.at[16], sibling)
    swap.start()
    swap.wait()
    res[chip] = mine[...] + other[...]

    def share(k):
        target = lax.rem(chip + k, 16)
        return remote(res.at[chip], res.at[chip], fsend.at[k - 1], frecv.at[chip], (t, target * 2 + h))

    def share_start(k, carry):
        share(k).start()
        return carry

    lax.fori_loop(1, 16, share_start, 0)

    def drain_hands(k, carry):
        remote(rown.at[k], rown.at[k], xsend.at[k], xrecv.at[0], sibling).wait_send()
        return carry

    lax.fori_loop(0, 32, drain_hands, 0)

    def share_wait(k, carry):
        who = lax.rem(chip + k, 16)
        share(k).wait_send()
        remote(res.at[who], res.at[who], fsend.at[k - 1], frecv.at[who], sibling).wait_recv()
        return carry

    lax.fori_loop(1, 16, share_wait, 0)
    lane = lax.broadcasted_iota(jnp.int32, (8, NEV), 1)
    gathered = zero
    for n in range(NOP):
        gathered = jnp.where(lane == n, res[n], gathered)
    out[...] = gathered


def on_device(sink_elem, source_elem, peram, pair_list, spin_sets):
    gathered = pl.pallas_call(
        kernel,
        name="correlate",
        out_shape=jax.ShapeDtypeStruct((8, NEV), F32),
        in_specs=[
            pl.BlockSpec(memory_space=pltpu.SMEM),
            pl.BlockSpec(memory_space=pltpu.SMEM),
            pl.BlockSpec(memory_space=pl.ANY),
            pl.BlockSpec(memory_space=pl.ANY),
            pl.BlockSpec(memory_space=pl.ANY),
        ],
        out_specs=pl.BlockSpec(memory_space=pltpu.VMEM),
        scratch_shapes=[
            pltpu.VMEM((2, NEV, NEV * NEV), BF16),
            pltpu.VMEM((NOP, NEV, 512), BF16),
            pltpu.VMEM((NOP, NEV, 512), BF16),
            pltpu.VMEM((30, NEV, 512), BF16),
            pltpu.VMEM((32, NEV, 512), BF16),
            pltpu.VMEM((32, NEV, 512), BF16),
            pltpu.VMEM((2, 4, 4, 32, NEV), BF16),
            pltpu.VMEM((3, 3, 2, 32, NEV), BF16),
            pltpu.VMEM((3, 2, 4, 32, NEV), BF16),
            pltpu.VMEM((2, 16 * NEV, NEV), F32),
            pltpu.VMEM((2 * NEV * NEV, NEV), F32),
            pltpu.VMEM((2 * NEV, 2 * NEV), F32),
            pltpu.VMEM((2 * NEV, 2 * NEV), BF16),
            pltpu.VMEM((2 * NEV, 2 * NEV), BF16),
            pltpu.VMEM((8, NEV), F32),
            pltpu.VMEM((8, NEV), F32),
            pltpu.VMEM((NOP, 8, NEV), F32),
            pltpu.SemaphoreType.DMA((12,)),
            pltpu.SemaphoreType.DMA((12,)),
            pltpu.SemaphoreType.DMA((12,)),
            pltpu.SemaphoreType.DMA((12,)),
            pltpu.SemaphoreType.DMA((12,)),
            pltpu.SemaphoreType.DMA((30,)),
            pltpu.SemaphoreType.DMA((32,)),
            pltpu.SemaphoreType.DMA((32,)),
            pltpu.SemaphoreType.DMA((32,)),
            pltpu.SemaphoreType.DMA((16,)),
            pltpu.SemaphoreType.DMA((17,)),
        ],
        compiler_params=pltpu.CompilerParams(
            collective_id=0, has_side_effects=True, vmem_limit_bytes=56 * 2**20
        ),
    )(pair_list.T, spin_sets.T, sink_elem, source_elem.reshape(2, TSRC, NOP, NEV, source_elem.shape[3]), peram)
    return gathered[:4, :NOP].reshape(2, 1, TSRC, NOP, 1)


def solution(mesh):
    in_specs = (
        P(None, "tm", "op", None),
        P(None, None, None, "op"),
        P(None, "tm", None, "op", None),
        P(),
        P(),
    )
    out_specs = P(None, "tm", None, None, None)
    return jax.shard_map(on_device, mesh=mesh, in_specs=in_specs, out_specs=out_specs, check_vma=False)
```

```python
import functools

import jax
import jax.numpy as jnp
from jax import lax
from jax.experimental import pallas as pl
from jax.experimental.pallas import tpu as pltpu
from jax.sharding import PartitionSpec as P

NEV = 128
NOP = 16
TSRC = 2
MESH = pl.DeviceIdType.MESH
BF16 = jnp.bfloat16
F32 = jnp.float32

XJ = 64
YP = 4
OUT = 12
EARLY = (4, 6)

ORDER = [
    (0, 1), (1, 0), (0, 3), (3, 0), (1, 1), (3, 3), (1, 3), (3, 1),
    (2, 0), (0, 2), (2, 2), (1, 2), (2, 1), (3, 2), (2, 3),
]
PACKED_Y = sum(dy * 4**k for k, (dy, dz) in enumerate(ORDER))
PACKED_Z = sum(dz * 4**k for k, (dy, dz) in enumerate(ORDER))


def kernel(
    pair_ref, spin_ref, sink, source, peram, out,
    phi, sown, ssib, sbuf, rown, rnb, taub, tout, tsel, xbuf, ybuf, pacc, t2m, t3m, mine, other, res,
    lsem, bsend, brecv, tsend, trecv, ssem, rsem, xsend, xrecv, fsend, frecv,
):
    t, o = lax.axis_index("tm"), lax.axis_index("op")
    h, chip = lax.rem(o, 2), lax.div(o, 2)
    y, z = lax.div(chip, 4), lax.rem(chip, 4)
    par = lax.rem(t, 2)
    sibling = (t, o + 1 - 2 * h)

    def at(y2, z2):
        return (t, (y2 * 4 + z2) * 2 + h)

    def beside(g):
        return (lax.rem(t + (1 - 2 * par) * (1 - 2 * g) + 4, 4), o)

    def remote(src, dst, send, recv, device):
        return pltpu.make_async_remote_copy(
            src_ref=src, dst_ref=dst, send_sem=send, recv_sem=recv, device_id=device, device_id_type=MESH
        )

    my_rows = pl.ds(pl.multiple_of(h * 64, 64), 64)

    local = []
    my_tau = pl.ds(pl.multiple_of(h * 16, 16), 16)
    for c in range(2):
        some = pl.ds(c * 8, 8)
        local.append(pltpu.make_async_copy(source.at[par, h, some], sown.at[some], lsem.at[c]))
    for c in range(2):
        local.append(pltpu.make_async_copy(sink.at[c, 0], phi.at[c, my_rows], lsem.at[2 + c]))
    for c in range(2):
        for b in range(4):
            local.append(
                pltpu.make_async_copy(
                    peram.at[c, 0, h, :, b * NEV : (b + 1) * NEV], taub.at[y, c, b, my_tau], lsem.at[4 + 4 * c + b]
                )
            )
    for copy in local:
        copy.start()

    barrier = pltpu.get_barrier_semaphore()

    def greet(k, carry):
        other_chip = lax.rem(chip + k, 16)
        pl.semaphore_signal(barrier, inc=1, device_id=(t, other_chip * 2 + h), device_id_type=MESH)
        return carry

    lax.fori_loop(1, 16, greet, 0)
    pl.semaphore_signal(barrier, inc=1, device_id=sibling, device_id_type=MESH)
    for g in range(2):
        pl.semaphore_signal(barrier, inc=1, device_id=beside(g), device_id_type=MESH)
    pl.semaphore_wait(barrier, 18)

    across = []
    for c in range(2):
        some = pl.ds(c * 8, 8)
        across.append(remote(source.at[par, 1 - h, some], ssib.at[some], bsend.at[c], brecv.at[c], sibling))
    for c in range(2):
        across.append(remote(sink.at[c, 0], phi.at[c, my_rows], bsend.at[2 + c], brecv.at[2 + c], sibling))
    for c in range(2):
        for b in range(4):
            n = 4 + 4 * c + b
            across.append(
                remote(
                    peram.at[c, 0, 1 - h, :, b * NEV : (b + 1) * NEV], taub.at[y, c, b, my_tau],
                    bsend.at[n], brecv.at[n], sibling,
                )
            )
    for copy in across[4:] + across[:4]:
        copy.start()

    first, second = [], []
    for d in range(1, 4):
        y2, z2 = lax.rem(y + d, 4), lax.rem(z + d, 4)
        first.append(remote(taub.at[y], taub.at[y], tsend.at[d - 1], trecv.at[d - 1], at(y2, z)))
        second.append(remote(tout.at[d - 1], tsel.at[z], tsend.at[d + 2], trecv.at[d + 2], at(y, z2)))

    def spread_rows():
        for n in range(4, 12):
            local[n].wait()
            across[n].wait_recv()
        for copy in first:
            copy.start()

    def pick(d, n, c):
        target = y * 4 + lax.rem(z + d, 4)
        return taub[spin_ref[n, target], c, spin_ref[n, pair_ref[0, target]]]

    def spread_blocks():
        for copy in first:
            copy.wait_recv()
        for d in range(1, 4):
            for n in range(3):
                for c in range(2):
                    tout[d - 1, n, c] = pick(d, n, c)
            second[d - 1].start()
        for n in range(3):
            for c in range(2):
                tsel[z, n, c] = pick(0, n, c)

    def hand_on(slot, g):
        return remote(rown.at[slot], rnb.at[slot], xsend.at[slot], xrecv.at[slot], beside(g))

    def advance(order):
        return tuple(lax.div(digits, 4) + lax.rem(digits, 4) * 4**14 for digits in order)

    def half_of(m):
        return lax.rem(h + lax.div(m, 15), 2)

    def serve(m, order):
        target = lax.rem(y + lax.rem(order[0], 4), 4) * 4 + lax.rem(z + lax.rem(order[1], 4), 4)
        q = pair_ref[0, target]

        @pl.when(m < 15)
        def _own():
            sbuf[m] = sown[q]

        @pl.when(m >= 15)
        def _sib():
            sbuf[m] = ssib[q]

        place = chip * 2 + half_of(m)
        remote(sbuf.at[m], rown.at[place], ssem.at[m], rsem.at[place], (t, target * 2 + h)).start()
        return advance(order)

    def keep(p, tiles):
        q = pair_ref[0, chip]
        g = lax.rem(h + p, 2)
        rown[chip * 2 + g] = tiles[q]
        hand_on(chip * 2 + g, g).start()

    def slot_of(m, order):
        from_y, from_z = lax.rem(y + 4 - lax.rem(order[0], 4), 4), lax.rem(z + 4 - lax.rem(order[1], 4), 4)
        return (from_y * 4 + from_z) * 2 + half_of(m)

    def pump(n, orders):
        coming, going = orders
        slot = slot_of(n, coming)
        remote(rown.at[slot], rown.at[slot], xsend.at[slot], rsem.at[slot], sibling).wait_recv()
        hand_on(slot, half_of(n)).start()

        @pl.when(n < 30 - OUT)
        def _more():
            serve(n + OUT, going)

        return advance(coming), advance(going)

    start = (jnp.int32(PACKED_Y), jnp.int32(PACKED_Z))
    for c in range(2):
        local[c].wait()
    keep(0, sown)
    going = lax.fori_loop(0, OUT, serve, start)
    spread_rows()
    for c in range(2):
        across[c].wait_recv()
    keep(1, ssib)
    orders = lax.fori_loop(0, EARLY[0], pump, (start, going))
    spread_blocks()
    orders = lax.fori_loop(EARLY[0], EARLY[0] + EARLY[1], pump, orders)

    for copy in second:
        copy.wait_recv()

    def block(c, n):
        return jnp.concatenate([tsel[k, n, c] for k in range(4)], axis=0)

    third_re, third_im = block(0, 2), block(1, 2)
    t3m[...] = jnp.concatenate(
        [jnp.concatenate([third_re, third_im], axis=1), jnp.concatenate([-third_im, third_re], axis=1)], axis=0
    )
    second_re, second_im = block(0, 1).astype(F32).T, block(1, 1).astype(F32).T
    t2m[...] = jnp.concatenate(
        [jnp.concatenate([second_re, -second_im], axis=1), jnp.concatenate([second_im, second_re], axis=1)], axis=0
    ).astype(BF16)
    for c in range(2):
        local[2 + c].wait()
        across[2 + c].wait_recv()

    def rows16(ic, orders):
        n = EARLY[0] + EARLY[1] + ic * 2
        i0 = pl.multiple_of(ic * 16, 16)

        def x_step(jb, inner):
            rows = []
            for jj in range(XJ):
                cols = pl.ds(pl.multiple_of((jb * XJ + jj) * NEV, NEV), NEV)
                rows.append(jnp.concatenate([phi[c, pl.ds(i0, 16), cols] for c in range(2)], axis=1))
            x = jnp.dot(jnp.concatenate(rows, axis=0), t3m[...], preferred_element_type=F32)
            place = pl.ds(pl.multiple_of(jb * (XJ * 16), XJ * 16), XJ * 16)
            xbuf[0, place, :] = x[:, :NEV]
            xbuf[1, place, :] = x[:, NEV:]
            return inner

        lax.fori_loop(0, NEV // XJ, x_step, 0)
        orders = pump(n, orders)

        def y_step(iq, inner):
            for ip in range(YP):
                first_i = iq * (2 * YP) + 2 * ip
                parts = []
                for c in range(2):
                    parts.append(
                        jnp.concatenate(
                            [xbuf[c, pl.ds(first_i + e, NEV, stride=16), :].astype(BF16) for e in range(2)], axis=1
                        )
                    )
                value = jnp.dot(t2m[...], jnp.concatenate(parts, axis=0), preferred_element_type=F32)
                for e in range(2):
                    place = pl.ds(pl.multiple_of((ic * 16 + first_i + e) * 256, 256), 256)
                    ybuf[place, :] = value[:, e * NEV : (e + 1) * NEV]
            return inner

        lax.fori_loop(0, 8 // YP, y_step, 0)
        return pump(n + 1, orders)

    orders = lax.fori_loop(0, 8, rows16, orders)

    def contract(slots):
        left, right = [[], []], [[], []]
        for slot in slots:
            for c in range(2):
                for jj in range(4):
                    left[c].append(ybuf[pl.ds(c * NEV + slot * 4 + jj, NEV, stride=256), :].astype(BF16))
            right[0].append(rown[slot])
            right[1].append(rnb[slot])
        left, right = (
            jnp.concatenate([jnp.concatenate(part, axis=1) for part in parts], axis=0) for parts in (left, right)
        )
        return lax.dot_general(left, right, (((1,), (1,)), ((), ())), preferred_element_type=F32)

    def handed(slot):
        remote(rnb.at[slot], rnb.at[slot], xsend.at[slot], xrecv.at[slot], sibling).wait_recv()

    own, nxt = chip * 2 + h, chip * 2 + 1 - h
    handed(own)
    handed(nxt)
    pacc[...] = contract([own, nxt])

    def main(k, carry):
        orders, order = carry
        n = EARLY[0] + EARLY[1] + 16 + k

        @pl.when(n < 30)
        def _last():
            pump(n, orders)

        a, order = slot_of(2 * k, order), advance(order)
        b, order = slot_of(2 * k + 1, order), advance(order)
        handed(a)
        handed(b)
        pacc[...] += contract([a, b])
        return (advance(orders[0]), advance(orders[1])), order

    lax.fori_loop(0, 15, main, (orders, start))

    for copy in across + first + second:
        copy.wait_send()

    def drain_sends(k, inner):
        remote(sbuf.at[k], sbuf.at[k], ssem.at[k], xrecv.at[0], sibling).wait_send()
        return inner

    lax.fori_loop(0, 30, drain_sends, 0)

    first_re, first_im = block(0, 0).astype(F32), block(1, 0).astype(F32)
    fetched, given = pacc[:, :NEV], pacc[:, NEV:]
    with_re, with_im = jnp.where(par == 0, fetched, given), jnp.where(par == 0, given, fetched)
    m_re = with_re[:NEV] + with_im[NEV:]
    m_im = with_re[NEV:] - with_im[:NEV]

    def total(v):
        return jnp.sum(jnp.sum(v, axis=0, keepdims=True), axis=1, keepdims=True) * (1.0 / float(NEV**3))

    c_re, c_im = total(first_re * m_re - first_im * m_im), total(first_re * m_im + first_im * m_re)
    row = lax.broadcasted_iota(jnp.int32, (8, NEV), 0)
    zero = jnp.zeros((8, NEV), F32)
    mine[...] = jnp.where(row == h, zero + c_re, jnp.where(row == 2 + h, zero + c_im, zero))
    swap = remote(mine, other, fsend.at[15], frecv.at[16], sibling)
    swap.start()
    swap.wait()
    res[chip] = mine[...] + other[...]

    def share(k):
        target = lax.rem(chip + k, 16)
        return remote(res.at[chip], res.at[chip], fsend.at[k - 1], frecv.at[chip], (t, target * 2 + h))

    def share_start(k, carry):
        share(k).start()
        return carry

    lax.fori_loop(1, 16, share_start, 0)

    def drain_hands(k, carry):
        remote(rown.at[k], rown.at[k], xsend.at[k], xrecv.at[0], sibling).wait_send()
        return carry

    lax.fori_loop(0, 32, drain_hands, 0)

    def share_wait(k, carry):
        who = lax.rem(chip + k, 16)
        share(k).wait_send()
        remote(res.at[who], res.at[who], fsend.at[k - 1], frecv.at[who], sibling).wait_recv()
        return carry

    lax.fori_loop(1, 16, share_wait, 0)
    lane = lax.broadcasted_iota(jnp.int32, (8, NEV), 1)
    gathered = zero
    for n in range(NOP):
        gathered = jnp.where(lane == n, res[n], gathered)
    out[...] = gathered


def on_device(sink_elem, source_elem, peram, pair_list, spin_sets):
    gathered = pl.pallas_call(
        kernel,
        name="correlate",
        out_shape=jax.ShapeDtypeStruct((8, NEV), F32),
        in_specs=[
            pl.BlockSpec(memory_space=pltpu.SMEM),
            pl.BlockSpec(memory_space=pltpu.SMEM),
            pl.BlockSpec(memory_space=pl.ANY),
            pl.BlockSpec(memory_space=pl.ANY),
            pl.BlockSpec(memory_space=pl.ANY),
        ],
        out_specs=pl.BlockSpec(memory_space=pltpu.VMEM),
        scratch_shapes=[
            pltpu.VMEM((2, NEV, NEV * NEV), BF16),
            pltpu.VMEM((NOP, NEV, 512), BF16),
            pltpu.VMEM((NOP, NEV, 512), BF16),
            pltpu.VMEM((30, NEV, 512), BF16),
            pltpu.VMEM((32, NEV, 512), BF16),
            pltpu.VMEM((32, NEV, 512), BF16),
            pltpu.VMEM((4, 2, 4, 32, NEV), BF16),
            pltpu.VMEM((3, 3, 2, 32, NEV), BF16),
            pltpu.VMEM((4, 3, 2, 32, NEV), BF16),
            pltpu.VMEM((2, 16 * NEV, NEV), F32),
            pltpu.VMEM((2 * NEV * NEV, NEV), F32),
            pltpu.VMEM((2 * NEV, 2 * NEV), F32),
            pltpu.VMEM((2 * NEV, 2 * NEV), BF16),
            pltpu.VMEM((2 * NEV, 2 * NEV), BF16),
            pltpu.VMEM((8, NEV), F32),
            pltpu.VMEM((8, NEV), F32),
            pltpu.VMEM((NOP, 8, NEV), F32),
            pltpu.SemaphoreType.DMA((12,)),
            pltpu.SemaphoreType.DMA((12,)),
            pltpu.SemaphoreType.DMA((12,)),
            pltpu.SemaphoreType.DMA((12,)),
            pltpu.SemaphoreType.DMA((12,)),
            pltpu.SemaphoreType.DMA((30,)),
            pltpu.SemaphoreType.DMA((32,)),
            pltpu.SemaphoreType.DMA((32,)),
            pltpu.SemaphoreType.DMA((32,)),
            pltpu.SemaphoreType.DMA((16,)),
            pltpu.SemaphoreType.DMA((17,)),
        ],
        compiler_params=pltpu.CompilerParams(
            collective_id=0, has_side_effects=True, vmem_limit_bytes=56 * 2**20
        ),
    )(pair_list.T, spin_sets.T, sink_elem, source_elem.reshape(2, TSRC, NOP, NEV, source_elem.shape[3]), peram)
    return gathered[:4, :NOP].reshape(2, 1, TSRC, NOP, 1)


def solution(mesh):
    in_specs = (
        P(None, "tm", "op", None),
        P(None, None, None, "op"),
        P(None, "tm", None, "op", None),
        P(),
        P(),
    )
    out_specs = P(None, "tm", None, None, None)
    return jax.shard_map(on_device, mesh=mesh, in_specs=in_specs, out_specs=out_specs, check_vma=False)
```

```python
import functools

import jax
import jax.numpy as jnp
from jax import lax
from jax.experimental import pallas as pl
from jax.experimental.pallas import tpu as pltpu
from jax.sharding import PartitionSpec as P

NEV = 128
NOP = 16
TSRC = 2
MESH = pl.DeviceIdType.MESH
BF16 = jnp.bfloat16
F32 = jnp.float32

XJ = 64
YP = 4
OUT = 12
EARLY = (4, 6)

ORDER = [
    (0, 1), (1, 0), (0, 3), (3, 0), (1, 1), (3, 3), (1, 3), (3, 1),
    (2, 0), (0, 2), (2, 2), (1, 2), (2, 1), (3, 2), (2, 3),
]
PACKED_Y = sum(dy * 4**k for k, (dy, dz) in enumerate(ORDER))
PACKED_Z = sum(dz * 4**k for k, (dy, dz) in enumerate(ORDER))


def kernel(
    pair_ref, spin_ref, sink, source, peram, out,
    phi, sown, ssib, sbuf, rown, rnb, taub, tout, tsel, xbuf, ybuf, pacc, t2m, t3m, mine, other, res,
    lsem, bsend, brecv, tsend, trecv, ssem, rsem, xsend, xrecv, fsend, frecv,
):
    t, o = lax.axis_index("tm"), lax.axis_index("op")
    h, chip = lax.rem(o, 2), lax.div(o, 2)
    y, z = lax.div(chip, 4), lax.rem(chip, 4)
    par = lax.rem(t, 2)
    sibling = (t, o + 1 - 2 * h)

    def at(y2, z2):
        return (t, (y2 * 4 + z2) * 2 + h)

    def beside(g):
        return (lax.rem(t + (1 - 2 * par) * (1 - 2 * g) + 4, 4), o)

    def remote(src, dst, send, recv, device):
        return pltpu.make_async_remote_copy(
            src_ref=src, dst_ref=dst, send_sem=send, recv_sem=recv, device_id=device, device_id_type=MESH
        )

    my_rows = pl.ds(pl.multiple_of(h * 64, 64), 64)

    local = []
    my_tau = pl.ds(pl.multiple_of(h * 16, 16), 16)
    for c in range(2):
        some = pl.ds(c * 8, 8)
        local.append(pltpu.make_async_copy(source.at[par, h, some], sown.at[some], lsem.at[c]))
    for c in range(2):
        local.append(pltpu.make_async_copy(sink.at[c, 0], phi.at[c, my_rows], lsem.at[2 + c]))
    for c in range(2):
        for b in range(4):
            local.append(
                pltpu.make_async_copy(
                    peram.at[c, 0, h, :, b * NEV : (b + 1) * NEV], taub.at[y, c, b, my_tau], lsem.at[4 + 4 * c + b]
                )
            )
    for copy in local:
        copy.start()

    barrier = pltpu.get_barrier_semaphore()

    def greet(k, carry):
        other_chip = lax.rem(chip + k, 16)
        pl.semaphore_signal(barrier, inc=1, device_id=(t, other_chip * 2 + h), device_id_type=MESH)
        return carry

    lax.fori_loop(1, 16, greet, 0)
    pl.semaphore_signal(barrier, inc=1, device_id=sibling, device_id_type=MESH)
    for g in range(2):
        pl.semaphore_signal(barrier, inc=1, device_id=beside(g), device_id_type=MESH)
    pl.semaphore_wait(barrier, 18)

    across = []
    for c in range(2):
        some = pl.ds(c * 8, 8)
        across.append(remote(source.at[par, 1 - h, some], ssib.at[some], bsend.at[c], brecv.at[c], sibling))
    for c in range(2):
        across.append(remote(sink.at[c, 0], phi.at[c, my_rows], bsend.at[2 + c], brecv.at[2 + c], sibling))
    for c in range(2):
        for b in range(4):
            n = 4 + 4 * c + b
            across.append(
                remote(
                    peram.at[c, 0, 1 - h, :, b * NEV : (b + 1) * NEV], taub.at[y, c, b, my_tau],
                    bsend.at[n], brecv.at[n], sibling,
                )
            )
    for copy in across[4:] + across[:4]:
        copy.start()

    first, second = [], []
    for d in range(1, 4):
        y2, z2 = lax.rem(y + d, 4), lax.rem(z + d, 4)
        first.append(remote(taub.at[y], taub.at[y], tsend.at[d - 1], trecv.at[d - 1], at(y2, z)))
        second.append(remote(tout.at[d - 1], tsel.at[z], tsend.at[d + 2], trecv.at[d + 2], at(y, z2)))

    def spread_rows():
        for n in range(4, 12):
            local[n].wait()
            across[n].wait_recv()
        for copy in first:
            copy.start()

    def pick(d, n, c):
        target = y * 4 + lax.rem(z + d, 4)
        return taub[spin_ref[n, target], c, spin_ref[n, pair_ref[0, target]]]

    def spread_blocks():
        for copy in first:
            copy.wait_recv()
        for d in range(1, 4):
            for n in range(3):
                for c in range(2):
                    tout[d - 1, n, c] = pick(d, n, c)
            second[d - 1].start()
        for n in range(3):
            for c in range(2):
                tsel[z, n, c] = pick(0, n, c)

    def hand_on(slot, g):
        return remote(rown.at[slot], rnb.at[slot], xsend.at[slot], xrecv.at[slot], beside(g))

    def advance(order):
        return tuple(lax.div(digits, 4) + lax.rem(digits, 4) * 4**14 for digits in order)

    def half_of(m):
        return lax.rem(h + lax.div(m, 15), 2)

    def serve(m, order):
        target = lax.rem(y + lax.rem(order[0], 4), 4) * 4 + lax.rem(z + lax.rem(order[1], 4), 4)
        q = pair_ref[0, target]

        @pl.when(m < 15)
        def _own():
            sbuf[m] = sown[q]

        @pl.when(m >= 15)
        def _sib():
            sbuf[m] = ssib[q]

        place = chip * 2 + half_of(m)
        remote(sbuf.at[m], rown.at[place], ssem.at[m], rsem.at[place], (t, target * 2 + h)).start()
        return advance(order)

    def keep(p, tiles):
        q = pair_ref[0, chip]
        g = lax.rem(h + p, 2)
        rown[chip * 2 + g] = tiles[q]
        hand_on(chip * 2 + g, g).start()

    def slot_of(m, order):
        from_y, from_z = lax.rem(y + 4 - lax.rem(order[0], 4), 4), lax.rem(z + 4 - lax.rem(order[1], 4), 4)
        return (from_y * 4 + from_z) * 2 + half_of(m)

    def pump(n, orders):
        coming, going = orders
        slot = slot_of(n, coming)
        remote(rown.at[slot], rown.at[slot], xsend.at[slot], rsem.at[slot], sibling).wait_recv()
        hand_on(slot, half_of(n)).start()

        @pl.when(n < 30 - OUT)
        def _more():
            serve(n + OUT, going)

        return advance(coming), advance(going)

    start = (jnp.int32(PACKED_Y), jnp.int32(PACKED_Z))
    for c in range(2):
        local[c].wait()
    keep(0, sown)
    going = lax.fori_loop(0, OUT, serve, start)
    spread_rows()
    for c in range(2):
        across[c].wait_recv()
    keep(1, ssib)
    orders = lax.fori_loop(0, EARLY[0], pump, (start, going))
    spread_blocks()
    orders = lax.fori_loop(EARLY[0], EARLY[0] + EARLY[1], pump, orders)

    for copy in second:
        copy.wait_recv()

    def block(c, n):
        return jnp.concatenate([tsel[k, n, c] for k in range(4)], axis=0)

    third_re, third_im = block(0, 2), block(1, 2)
    t3m[...] = jnp.concatenate(
        [jnp.concatenate([third_re, third_im], axis=1), jnp.concatenate([-third_im, third_re], axis=1)], axis=0
    )
    second_re, second_im = block(0, 1).astype(F32).T, block(1, 1).astype(F32).T
    t2m[...] = jnp.concatenate(
        [jnp.concatenate([second_re, -second_im], axis=1), jnp.concatenate([second_im, second_re], axis=1)], axis=0
    ).astype(BF16)
    for c in range(2):
        local[2 + c].wait()
        across[2 + c].wait_recv()

    def rows16(ic, orders):
        n = EARLY[0] + EARLY[1] + ic * 2
        i0 = pl.multiple_of(ic * 16, 16)

        def x_step(jb, inner):
            rows = []
            for jj in range(XJ):
                cols = pl.ds(pl.multiple_of((jb * XJ + jj) * NEV, NEV), NEV)
                rows.append(jnp.concatenate([phi[c, pl.ds(i0, 16), cols] for c in range(2)], axis=1))
            x = jnp.dot(jnp.concatenate(rows, axis=0), t3m[...], preferred_element_type=F32)
            place = pl.ds(pl.multiple_of(jb * (XJ * 16), XJ * 16), XJ * 16)
            xbuf[0, place, :] = x[:, :NEV]
            xbuf[1, place, :] = x[:, NEV:]
            return inner

        lax.fori_loop(0, NEV // XJ, x_step, 0)
        orders = pump(n, orders)

        def y_step(iq, inner):
            for ip in range(YP):
                first_i = iq * (2 * YP) + 2 * ip
                parts = []
                for c in range(2):
                    parts.append(
                        jnp.concatenate(
                            [xbuf[c, pl.ds(first_i + e, NEV, stride=16), :].astype(BF16) for e in range(2)], axis=1
                        )
                    )
                value = jnp.dot(t2m[...], jnp.concatenate(parts, axis=0), preferred_element_type=F32)
                for e in range(2):
                    place = pl.ds(pl.multiple_of((ic * 16 + first_i + e) * 256, 256), 256)
                    ybuf[place, :] = value[:, e * NEV : (e + 1) * NEV]
            return inner

        lax.fori_loop(0, 8 // YP, y_step, 0)
        return pump(n + 1, orders)

    orders = lax.fori_loop(0, 8, rows16, orders)

    def contract(slots):
        left, right = [[], []], [[], []]
        for slot in slots:
            for c in range(2):
                for jj in range(4):
                    left[c].append(ybuf[pl.ds(c * NEV + slot * 4 + jj, NEV, stride=256), :].astype(BF16))
            right[0].append(rown[slot])
            right[1].append(rnb[slot])
        left, right = (
            jnp.concatenate([jnp.concatenate(part, axis=1) for part in parts], axis=0) for parts in (left, right)
        )
        return lax.dot_general(left, right, (((1,), (1,)), ((), ())), preferred_element_type=F32)

    def handed(slot):
        remote(rnb.at[slot], rnb.at[slot], xsend.at[slot], xrecv.at[slot], sibling).wait_recv()

    own, nxt = chip * 2 + h, chip * 2 + 1 - h
    handed(own)
    handed(nxt)
    pacc[...] = contract([own, nxt])

    def main(k, carry):
        orders, order = carry
        n = EARLY[0] + EARLY[1] + 16 + k

        @pl.when(n < 30)
        def _last():
            pump(n, orders)

        a, order = slot_of(2 * k, order), advance(order)
        b, order = slot_of(2 * k + 1, order), advance(order)
        handed(a)
        handed(b)
        pacc[...] += contract([a, b])
        return (advance(orders[0]), advance(orders[1])), order

    lax.fori_loop(0, 15, main, (orders, start))

    for copy in across + first + second:
        copy.wait_send()

    def drain_sends(k, inner):
        remote(sbuf.at[k], sbuf.at[k], ssem.at[k], xrecv.at[0], sibling).wait_send()
        return inner

    lax.fori_loop(0, 30, drain_sends, 0)

    first_re, first_im = block(0, 0).astype(F32), block(1, 0).astype(F32)
    fetched, given = pacc[:, :NEV], pacc[:, NEV:]
    with_re, with_im = jnp.where(par == 0, fetched, given), jnp.where(par == 0, given, fetched)
    m_re = with_re[:NEV] + with_im[NEV:]
    m_im = with_re[NEV:] - with_im[:NEV]

    def total(v):
        return jnp.sum(jnp.sum(v, axis=0, keepdims=True), axis=1, keepdims=True) * (1.0 / float(NEV**3))

    c_re, c_im = total(first_re * m_re - first_im * m_im), total(first_re * m_im + first_im * m_re)
    row = lax.broadcasted_iota(jnp.int32, (8, NEV), 0)
    zero = jnp.zeros((8, NEV), F32)
    mine[...] = jnp.where(row == h, zero + c_re, jnp.where(row == 2 + h, zero + c_im, zero))
    swap = remote(mine, other, fsend.at[15], frecv.at[16], sibling)
    swap.start()
    swap.wait()
    res[chip] = mine[...] + other[...]

    def share(k):
        target = lax.rem(chip + k, 16)
        return remote(res.at[chip], res.at[chip], fsend.at[k - 1], frecv.at[chip], (t, target * 2 + h))

    def share_start(k, carry):
        share(k).start()
        return carry

    lax.fori_loop(1, 16, share_start, 0)

    def drain_hands(k, carry):
        remote(rown.at[k], rown.at[k], xsend.at[k], xrecv.at[0], sibling).wait_send()
        return carry

    lax.fori_loop(0, 32, drain_hands, 0)

    def share_wait(k, carry):
        who = lax.rem(chip + k, 16)
        share(k).wait_send()
        remote(res.at[who], res.at[who], fsend.at[k - 1], frecv.at[who], sibling).wait_recv()
        return carry

    lax.fori_loop(1, 16, share_wait, 0)
    lane = lax.broadcasted_iota(jnp.int32, (8, NEV), 1)
    gathered = zero
    for n in range(NOP):
        gathered = jnp.where(lane == n, res[n], gathered)
    out[...] = gathered


def on_device(sink_elem, source_elem, peram, pair_list, spin_sets):
    gathered = pl.pallas_call(
        kernel,
        name="correlate",
        out_shape=jax.ShapeDtypeStruct((8, NEV), F32),
        in_specs=[
            pl.BlockSpec(memory_space=pltpu.SMEM),
            pl.BlockSpec(memory_space=pltpu.SMEM),
            pl.BlockSpec(memory_space=pl.ANY),
            pl.BlockSpec(memory_space=pl.ANY),
            pl.BlockSpec(memory_space=pl.ANY),
        ],
        out_specs=pl.BlockSpec(memory_space=pltpu.VMEM),
        scratch_shapes=[
            pltpu.VMEM((2, NEV, NEV * NEV), BF16),
            pltpu.VMEM((NOP, NEV, 512), BF16),
            pltpu.VMEM((NOP, NEV, 512), BF16),
            pltpu.VMEM((30, NEV, 512), BF16),
            pltpu.VMEM((32, NEV, 512), BF16),
            pltpu.VMEM((32, NEV, 512), BF16),
            pltpu.VMEM((4, 2, 4, 32, NEV), BF16),
            pltpu.VMEM((3, 3, 2, 32, NEV), BF16),
            pltpu.VMEM((4, 3, 2, 32, NEV), BF16),
            pltpu.VMEM((2, 16 * NEV + 16, NEV), F32),
            pltpu.VMEM((2 * NEV * NEV + 2 * NEV, NEV), F32),
            pltpu.VMEM((2 * NEV, 2 * NEV), F32),
            pltpu.VMEM((2 * NEV, 2 * NEV), BF16),
            pltpu.VMEM((2 * NEV, 2 * NEV), BF16),
            pltpu.VMEM((8, NEV), F32),
            pltpu.VMEM((8, NEV), F32),
            pltpu.VMEM((NOP, 8, NEV), F32),
            pltpu.SemaphoreType.DMA((12,)),
            pltpu.SemaphoreType.DMA((12,)),
            pltpu.SemaphoreType.DMA((12,)),
            pltpu.SemaphoreType.DMA((12,)),
            pltpu.SemaphoreType.DMA((12,)),
            pltpu.SemaphoreType.DMA((30,)),
            pltpu.SemaphoreType.DMA((32,)),
            pltpu.SemaphoreType.DMA((32,)),
            pltpu.SemaphoreType.DMA((32,)),
            pltpu.SemaphoreType.DMA((16,)),
            pltpu.SemaphoreType.DMA((17,)),
        ],
        compiler_params=pltpu.CompilerParams(
            collective_id=0, has_side_effects=True, vmem_limit_bytes=56 * 2**20
        ),
    )(pair_list.T, spin_sets.T, sink_elem, source_elem.reshape(2, TSRC, NOP, NEV, source_elem.shape[3]), peram)
    return gathered[:4, :NOP].reshape(2, 1, TSRC, NOP, 1)


def solution(mesh):
    in_specs = (
        P(None, "tm", "op", None),
        P(None, None, None, "op"),
        P(None, "tm", None, "op", None),
        P(),
        P(),
    )
    out_specs = P(None, "tm", None, None, None)
    return jax.shard_map(on_device, mesh=mesh, in_specs=in_specs, out_specs=out_specs, check_vma=False)
```

```python
import functools

import jax
import jax.numpy as jnp
from jax import lax
from jax.experimental import pallas as pl
from jax.experimental.pallas import tpu as pltpu
from jax.sharding import PartitionSpec as P

NEV = 128
NOP = 16
TSRC = 2
MESH = pl.DeviceIdType.MESH
BF16 = jnp.bfloat16
F32 = jnp.float32

XJ = 64
YP = 4
OUT = 12
EARLY = (4, 6)

ORDER = [
    (0, 1), (1, 0), (0, 3), (3, 0), (1, 1), (3, 3), (1, 3), (3, 1),
    (2, 0), (0, 2), (2, 2), (1, 2), (2, 1), (3, 2), (2, 3),
]
PACKED_Y = sum(dy * 4**k for k, (dy, dz) in enumerate(ORDER))
PACKED_Z = sum(dz * 4**k for k, (dy, dz) in enumerate(ORDER))


def kernel(
    pair_ref, spin_ref, sink, source, peram, out,
    phi, sown, ssib, sbuf, rown, rnb, taub, tout, tsel, xbuf, ybuf, pacc, t2m, t3m, mine, other, res,
    lsem, bsend, brecv, tsend, trecv, ssem, rsem, xsend, xrecv, fsend, frecv,
):
    t, o = lax.axis_index("tm"), lax.axis_index("op")
    h, chip = lax.rem(o, 2), lax.div(o, 2)
    y, z = lax.div(chip, 4), lax.rem(chip, 4)
    par = lax.rem(t, 2)
    sibling = (t, o + 1 - 2 * h)

    def at(y2, z2):
        return (t, (y2 * 4 + z2) * 2 + h)

    def beside(g):
        return (lax.rem(t + (1 - 2 * par) * (1 - 2 * g) + 4, 4), o)

    def remote(src, dst, send, recv, device):
        return pltpu.make_async_remote_copy(
            src_ref=src, dst_ref=dst, send_sem=send, recv_sem=recv, device_id=device, device_id_type=MESH
        )

    my_rows = pl.ds(pl.multiple_of(h * 64, 64), 64)

    local = []
    my_tau = pl.ds(pl.multiple_of(h * 16, 16), 16)
    for c in range(2):
        some = pl.ds(c * 8, 8)
        local.append(pltpu.make_async_copy(source.at[par, h, some], sown.at[some], lsem.at[c]))
    for c in range(2):
        local.append(pltpu.make_async_copy(sink.at[c, 0], phi.at[c, my_rows], lsem.at[2 + c]))
    for c in range(2):
        for b in range(4):
            local.append(
                pltpu.make_async_copy(
                    peram.at[c, 0, h, :, b * NEV : (b + 1) * NEV], taub.at[y, c, b, my_tau], lsem.at[4 + 4 * c + b]
                )
            )
    for copy in local:
        copy.start()

    barrier = pltpu.get_barrier_semaphore()

    def greet(k, carry):
        other_chip = lax.rem(chip + k, 16)
        pl.semaphore_signal(barrier, inc=1, device_id=(t, other_chip * 2 + h), device_id_type=MESH)
        return carry

    lax.fori_loop(1, 16, greet, 0)
    pl.semaphore_signal(barrier, inc=1, device_id=sibling, device_id_type=MESH)
    for g in range(2):
        pl.semaphore_signal(barrier, inc=1, device_id=beside(g), device_id_type=MESH)
    pl.semaphore_wait(barrier, 18)

    across = []
    for c in range(2):
        some = pl.ds(c * 8, 8)
        across.append(remote(source.at[par, 1 - h, some], ssib.at[some], bsend.at[c], brecv.at[c], sibling))
    for c in range(2):
        across.append(remote(sink.at[c, 0], phi.at[c, my_rows], bsend.at[2 + c], brecv.at[2 + c], sibling))
    for c in range(2):
        for b in range(4):
            n = 4 + 4 * c + b
            across.append(
                remote(
                    peram.at[c, 0, 1 - h, :, b * NEV : (b + 1) * NEV], taub.at[y, c, b, my_tau],
                    bsend.at[n], brecv.at[n], sibling,
                )
            )
    for copy in across[4:] + across[:4]:
        copy.start()

    first, second = [], []
    for d in range(1, 4):
        y2, z2 = lax.rem(y + d, 4), lax.rem(z + d, 4)
        first.append(remote(taub.at[y], taub.at[y], tsend.at[d - 1], trecv.at[d - 1], at(y2, z)))
        second.append(remote(tout.at[d - 1], tsel.at[z], tsend.at[d + 2], trecv.at[d + 2], at(y, z2)))

    def spread_rows():
        for n in range(4, 12):
            local[n].wait()
            across[n].wait_recv()
        for copy in first:
            copy.start()

    def pick(d, n, c):
        target = y * 4 + lax.rem(z + d, 4)
        return taub[spin_ref[n, target], c, spin_ref[n, pair_ref[0, target]]]

    def spread_blocks():
        for copy in first:
            copy.wait_recv()
        for d in range(1, 4):
            for n in range(3):
                for c in range(2):
                    tout[d - 1, n, c] = pick(d, n, c)
            second[d - 1].start()
        for n in range(3):
            for c in range(2):
                tsel[z, n, c] = pick(0, n, c)

    def hand_on(slot, g):
        return remote(rown.at[slot], rnb.at[slot], xsend.at[slot], xrecv.at[slot], beside(g))

    def advance(order):
        return tuple(lax.div(digits, 4) + lax.rem(digits, 4) * 4**14 for digits in order)

    def half_of(m):
        return lax.rem(h + lax.div(m, 15), 2)

    def serve(m, order):
        target = lax.rem(y + lax.rem(order[0], 4), 4) * 4 + lax.rem(z + lax.rem(order[1], 4), 4)
        q = pair_ref[0, target]

        @pl.when(m < 15)
        def _own():
            sbuf[m] = sown[q]

        @pl.when(m >= 15)
        def _sib():
            sbuf[m] = ssib[q]

        place = chip * 2 + half_of(m)
        remote(sbuf.at[m], rown.at[place], ssem.at[m], rsem.at[place], (t, target * 2 + h)).start()
        return advance(order)

    def keep(p, tiles):
        q = pair_ref[0, chip]
        g = lax.rem(h + p, 2)
        rown[chip * 2 + g] = tiles[q]
        hand_on(chip * 2 + g, g).start()

    def slot_of(m, order):
        from_y, from_z = lax.rem(y + 4 - lax.rem(order[0], 4), 4), lax.rem(z + 4 - lax.rem(order[1], 4), 4)
        return (from_y * 4 + from_z) * 2 + half_of(m)

    def pump(n, orders):
        coming, going = orders
        slot = slot_of(n, coming)
        remote(rown.at[slot], rown.at[slot], xsend.at[slot], rsem.at[slot], sibling).wait_recv()
        hand_on(slot, half_of(n)).start()

        @pl.when(n < 30 - OUT)
        def _more():
            serve(n + OUT, going)

        return advance(coming), advance(going)

    start = (jnp.int32(PACKED_Y), jnp.int32(PACKED_Z))
    for c in range(2):
        local[c].wait()
    keep(0, sown)
    going = lax.fori_loop(0, OUT, serve, start)
    spread_rows()
    for c in range(2):
        across[c].wait_recv()
    keep(1, ssib)
    orders = lax.fori_loop(0, EARLY[0], pump, (start, going))
    spread_blocks()
    orders = lax.fori_loop(EARLY[0], EARLY[0] + EARLY[1], pump, orders)

    for copy in second:
        copy.wait_recv()

    def block(c, n):
        return jnp.concatenate([tsel[k, n, c] for k in range(4)], axis=0)

    third_re, third_im = block(0, 2), block(1, 2)
    t3m[...] = jnp.concatenate(
        [jnp.concatenate([third_re, third_im], axis=1), jnp.concatenate([-third_im, third_re], axis=1)], axis=0
    )
    second_re, second_im = block(0, 1).astype(F32).T, block(1, 1).astype(F32).T
    t2m[...] = jnp.concatenate(
        [jnp.concatenate([second_re, -second_im], axis=1), jnp.concatenate([second_im, second_re], axis=1)], axis=0
    ).astype(BF16)
    for c in range(2):
        local[2 + c].wait()
        across[2 + c].wait_recv()

    def rows16(ic, orders):
        n = EARLY[0] + EARLY[1] + ic * 2
        i0 = pl.multiple_of(ic * 16, 16)

        def x_step(jb, inner):
            rows = []
            for jj in range(XJ):
                cols = pl.ds(pl.multiple_of((jb * XJ + jj) * NEV, NEV), NEV)
                rows.append(jnp.concatenate([phi[c, pl.ds(i0, 16), cols] for c in range(2)], axis=1))
            x = jnp.dot(jnp.concatenate(rows, axis=0), t3m[...], preferred_element_type=F32)
            place = pl.ds(pl.multiple_of(jb * (XJ * 16), XJ * 16), XJ * 16)
            xbuf[0, place, :] = x[:, :NEV]
            xbuf[1, place, :] = x[:, NEV:]
            return inner

        lax.fori_loop(0, NEV // XJ, x_step, 0)
        orders = pump(n, orders)

        def y_step(iq, inner):
            for ip in range(YP):
                first_i = iq * (2 * YP) + 2 * ip
                parts = []
                for c in range(2):
                    parts.append(
                        jnp.concatenate(
                            [xbuf[c, pl.ds(first_i + e, NEV, stride=16), :].astype(BF16) for e in range(2)], axis=1
                        )
                    )
                value = jnp.dot(t2m[...], jnp.concatenate(parts, axis=0), preferred_element_type=F32)
                for e in range(2):
                    place = pl.ds(pl.multiple_of((ic * 16 + first_i + e) * 256, 256), 256)
                    ybuf[place, :] = value[:, e * NEV : (e + 1) * NEV]
            return inner

        lax.fori_loop(0, 8 // YP, y_step, 0)
        return pump(n + 1, orders)

    orders = lax.fori_loop(0, 8, rows16, orders)

    def contract(slots):
        left, right = [[], []], [[], []]
        for slot in slots:
            for c in range(2):
                for jj in range(4):
                    left[c].append(ybuf[pl.ds(c * NEV + slot * 4 + jj, NEV, stride=256), :].astype(BF16))
            right[0].append(rown[slot])
            right[1].append(rnb[slot])
        left, right = (
            jnp.concatenate([jnp.concatenate(part, axis=1) for part in parts], axis=0) for parts in (left, right)
        )
        return lax.dot_general(left, right, (((1,), (1,)), ((), ())), preferred_element_type=F32)

    def handed(slot):
        remote(rnb.at[slot], rnb.at[slot], xsend.at[slot], xrecv.at[slot], sibling).wait_recv()

    own, nxt = chip * 2 + h, chip * 2 + 1 - h
    handed(own)
    handed(nxt)
    pacc[...] = contract([own, nxt])

    def main(k, carry):
        orders, order = carry
        n = EARLY[0] + EARLY[1] + 16 + k

        @pl.when(n < 30)
        def _last():
            pump(n, orders)

        a, order = slot_of(2 * k, order), advance(order)
        b, order = slot_of(2 * k + 1, order), advance(order)
        handed(a)
        handed(b)
        pacc[...] += contract([a, b])
        return (advance(orders[0]), advance(orders[1])), order

    lax.fori_loop(0, 15, main, (orders, start))

    first_re, first_im = block(0, 0).astype(F32), block(1, 0).astype(F32)
    fetched, given = pacc[:, :NEV], pacc[:, NEV:]
    with_re, with_im = jnp.where(par == 0, fetched, given), jnp.where(par == 0, given, fetched)
    m_re = with_re[:NEV] + with_im[NEV:]
    m_im = with_re[NEV:] - with_im[:NEV]

    def total(v):
        return jnp.sum(jnp.sum(v, axis=0, keepdims=True), axis=1, keepdims=True) * (1.0 / float(NEV**3))

    c_re, c_im = total(first_re * m_re - first_im * m_im), total(first_re * m_im + first_im * m_re)
    row = lax.broadcasted_iota(jnp.int32, (8, NEV), 0)
    zero = jnp.zeros((8, NEV), F32)
    mine[...] = jnp.where(row == h, zero + c_re, jnp.where(row == 2 + h, zero + c_im, zero))
    swap = remote(mine, other, fsend.at[15], frecv.at[16], sibling)
    swap.start()
    swap.wait()
    res[chip] = mine[...] + other[...]

    def share(k):
        target = lax.rem(chip + k, 16)
        return remote(res.at[chip], res.at[chip], fsend.at[k - 1], frecv.at[chip], (t, target * 2 + h))

    def share_start(k, carry):
        share(k).start()
        return carry

    lax.fori_loop(1, 16, share_start, 0)

    def drain_hands(k, carry):
        remote(rown.at[k], rown.at[k], xsend.at[k], xrecv.at[0], sibling).wait_send()
        return carry

    lax.fori_loop(0, 32, drain_hands, 0)

    for copy in across + first + second:
        copy.wait_send()

    def drain_sends(k, inner):
        remote(sbuf.at[k], sbuf.at[k], ssem.at[k], xrecv.at[0], sibling).wait_send()
        return inner

    lax.fori_loop(0, 30, drain_sends, 0)

    def share_wait(k, carry):
        who = lax.rem(chip + k, 16)
        share(k).wait_send()
        remote(res.at[who], res.at[who], fsend.at[k - 1], frecv.at[who], sibling).wait_recv()
        return carry

    lax.fori_loop(1, 16, share_wait, 0)
    lane = lax.broadcasted_iota(jnp.int32, (8, NEV), 1)
    gathered = zero
    for n in range(NOP):
        gathered = jnp.where(lane == n, res[n], gathered)
    out[...] = gathered


def on_device(sink_elem, source_elem, peram, pair_list, spin_sets):
    gathered = pl.pallas_call(
        kernel,
        name="correlate",
        out_shape=jax.ShapeDtypeStruct((8, NEV), F32),
        in_specs=[
            pl.BlockSpec(memory_space=pltpu.SMEM),
            pl.BlockSpec(memory_space=pltpu.SMEM),
            pl.BlockSpec(memory_space=pl.ANY),
            pl.BlockSpec(memory_space=pl.ANY),
            pl.BlockSpec(memory_space=pl.ANY),
        ],
        out_specs=pl.BlockSpec(memory_space=pltpu.VMEM),
        scratch_shapes=[
            pltpu.VMEM((2, NEV, NEV * NEV), BF16),
            pltpu.VMEM((NOP, NEV, 512), BF16),
            pltpu.VMEM((NOP, NEV, 512), BF16),
            pltpu.VMEM((30, NEV, 512), BF16),
            pltpu.VMEM((32, NEV, 512), BF16),
            pltpu.VMEM((32, NEV, 512), BF16),
            pltpu.VMEM((4, 2, 4, 32, NEV), BF16),
            pltpu.VMEM((3, 3, 2, 32, NEV), BF16),
            pltpu.VMEM((4, 3, 2, 32, NEV), BF16),
            pltpu.VMEM((2, 16 * NEV + 16, NEV), F32),
            pltpu.VMEM((2 * NEV * NEV + 2 * NEV, NEV), F32),
            pltpu.VMEM((2 * NEV, 2 * NEV), F32),
            pltpu.VMEM((2 * NEV, 2 * NEV), BF16),
            pltpu.VMEM((2 * NEV, 2 * NEV), BF16),
            pltpu.VMEM((8, NEV), F32),
            pltpu.VMEM((8, NEV), F32),
            pltpu.VMEM((NOP, 8, NEV), F32),
            pltpu.SemaphoreType.DMA((12,)),
            pltpu.SemaphoreType.DMA((12,)),
            pltpu.SemaphoreType.DMA((12,)),
            pltpu.SemaphoreType.DMA((12,)),
            pltpu.SemaphoreType.DMA((12,)),
            pltpu.SemaphoreType.DMA((30,)),
            pltpu.SemaphoreType.DMA((32,)),
            pltpu.SemaphoreType.DMA((32,)),
            pltpu.SemaphoreType.DMA((32,)),
            pltpu.SemaphoreType.DMA((16,)),
            pltpu.SemaphoreType.DMA((17,)),
        ],
        compiler_params=pltpu.CompilerParams(
            collective_id=0, has_side_effects=True, vmem_limit_bytes=56 * 2**20
        ),
    )(pair_list.T, spin_sets.T, sink_elem, source_elem.reshape(2, TSRC, NOP, NEV, source_elem.shape[3]), peram)
    return gathered[:4, :NOP].reshape(2, 1, TSRC, NOP, 1)


def solution(mesh):
    in_specs = (
        P(None, "tm", "op", None),
        P(None, None, None, "op"),
        P(None, "tm", None, "op", None),
        P(),
        P(),
    )
    out_specs = P(None, "tm", None, None, None)
    return jax.shard_map(on_device, mesh=mesh, in_specs=in_specs, out_specs=out_specs, check_vma=False)
```
